1024 devices in a mesh: dp: 8 (over x), pipe: 16 (over z, core), tensor: 8 (over y).
Axes of the slice: x: 8, y: 8, z: 8, core: 2. Of those that a mesh axis runs over, the one named last changes fastest.
Arguments:
- hidden: bfloat16 [1024, 8192], P(('dp', 'pipe'), 'tensor'), parts along dimension 0, may hold values from -15 to 15
- gain: float32 [8192], replicated, may hold values from 0.1 to 1.9
- lm_head: bfloat16 [79872, 8192], P(('pipe', 'tensor')), may hold values from -0.29831067 to 0.29831067
- targets: int32 [1024], P('dp'), parts along dimension 0, may hold values from 0 to 79871
- banned: int32 [79872], P(('pipe', 'tensor')), may hold values 0 or 1
Outputs:
- loss: float32 [1024], P(('dp', 'pipe')), parts along dimension 0
- grad_hidden: bfloat16 [1024, 8192], P(('dp', 'pipe'), 'tensor'), parts along dimension 0
The draws below stay inside these ranges and needn't reach their ends.
There are 8 independent parts, one for each index of `dp`. The reference program is written for one: setup_inputs(seed, part) draws one part's arguments, and reference() takes and returns one part's arrays. A program takes and returns all parts, laid end to end along the dimension named above; an argument that names none is the same for every part. Nothing has to cross between parts.
All inputs are finite; a program needn't handle non-finite values. No bound on the sum of `banned` on one device may be relied on, other than what follows from the above.
Results may differ from the reference program's by a relative error of at most 0.0056.
Values may be sent and summed in bfloat16 or wider, within the bound.
No kernel may reach another device: no remote copies, remote signals or barrier semaphores. Data moves between devices by JAX's collectives and lax.ppermute only.
A program may use at most 64 MiB of HBM per device.

```python
import math
import jax
import jax.numpy as jnp
from jax import lax

D = 8192
VOCAB = 79872
TOK = 128


def draw_hidden(key, part):
    first, second, third = jax.random.split(key, 3)
    row_scale = jnp.exp(jax.random.uniform(second, (TOK, 1), jnp.float32, math.log(0.02), math.log(0.2)))
    rise = jnp.exp(math.log(3.0) * jnp.arange(D, dtype=jnp.float32) / D)
    col_scale = jnp.exp(jax.random.uniform(third, (1, D), jnp.float32, math.log(0.4), math.log(4.0))) * rise[None, :]
    base = jnp.clip(jax.random.normal(first, (TOK, D), jnp.float32), -6.0, 6.0)
    value = base * row_scale * col_scale
    return jnp.clip(value, -15.0, 15.0).astype(jnp.bfloat16)


def draw_lm_head(key, part):
    first = jax.random.fold_in(key, 0)
    scale = 3.0 / math.sqrt(D)
    rise = 0.6 + 0.9 * jnp.arange(VOCAB, dtype=jnp.float32) / VOCAB
    base = jnp.clip(jax.random.normal(first, (VOCAB, D), jnp.float32), -6.0, 6.0)
    value = scale * base * rise[:, None]
    bound = 27.0 / math.sqrt(D)
    return jnp.clip(value, -bound, bound).astype(jnp.bfloat16)


def set_ends(values, stream_key, smallest, top_value):
    shape = values.shape
    spot = [jax.random.randint(jax.random.fold_in(stream_key, axis), (), 0, shape[axis]) for axis in range(len(shape))]
    values = values.at[tuple(spot)].set(smallest)
    longest = shape.index(max(shape))
    spot[longest] = (spot[longest] + 1) % shape[longest]
    return values.at[tuple(spot)].set(top_value)


def setup_inputs(seed: int = 0, part: int = 0) -> dict:
    seeds = jax.random.split(jax.random.key(seed), 6)
    part_keys = jax.random.split(jax.random.fold_in(seeds[5], part), 6)
    return {
        "hidden": draw_hidden(jax.random.fold_in(jax.random.fold_in(seeds[5], part), 71), part),
        "gain": jnp.clip(1.0 + 0.18 * jax.random.normal(seeds[1], (D,), jnp.float32), 0.1, 1.9),
        "lm_head": draw_lm_head(jax.random.fold_in(seeds[5], 71), part),
        "targets": set_ends(jax.random.randint(part_keys[3], (TOK,), 0, VOCAB), jax.random.fold_in(part_keys[3], 1), 0, VOCAB - 1).astype(jnp.int32),
        "banned": set_ends((jax.random.randint(seeds[4], (VOCAB,), 0, 8) < 1).astype(jnp.int32), jax.random.fold_in(seeds[4], 1), 0, 1),
    }


EPSILON = 1e-05

def reference(hidden, gain, lm_head, targets, banned):
    hidden_wide = hidden.astype(jnp.float32)
    inverse = lax.rsqrt(lax.optimization_barrier(jnp.mean(hidden_wide * hidden_wide, axis=1, keepdims=True)) + EPSILON)
    scaled = hidden_wide * inverse
    normed = (scaled * gain[None, :]).astype(jnp.bfloat16)
    logits = jnp.dot(normed, lm_head.T, preferred_element_type=jnp.float32)
    vocab_ids = jnp.arange(VOCAB, dtype=jnp.int32)
    is_target = vocab_ids[None, :] == targets[:, None]
    allowed = (banned[None, :] == 0) | is_target
    row_max = lax.optimization_barrier(jnp.max(jnp.where(allowed, logits, -1e+30), axis=1))
    shifted = jnp.where(allowed, jnp.exp(logits - row_max[:, None]), 0.0)
    sum_exp = lax.optimization_barrier(jnp.sum(shifted, axis=1))
    target_logit = lax.optimization_barrier(jnp.sum(jnp.where(is_target, logits, 0.0), axis=1))
    loss = row_max + jnp.log(sum_exp) - target_logit
    probs = shifted / sum_exp[:, None]
    dlogits = (probs - is_target.astype(jnp.float32)).astype(jnp.bfloat16)
    grad_normed = jnp.dot(dlogits, lm_head, preferred_element_type=jnp.float32)
    gated = grad_normed * gain[None, :]
    inner = lax.optimization_barrier(jnp.mean(gated * scaled, axis=1, keepdims=True))
    grad_hidden = (inverse * (gated - scaled * inner)).astype(jnp.bfloat16)
    return (loss, grad_hidden)
```

```python
import jax
import jax.numpy as jnp
from jax import lax
from jax.sharding import Mesh
from jax.sharding import PartitionSpec as P

EPSILON = 1e-05
LOWEST = -1e30
CORES = 2
PLANE = ("z", "tensor")


def swap_cores(values):
    return lax.ppermute(values, "core", [(0, 1), (1, 0)])


def local(hidden, gain, lm_head, targets, banned):
    z_count = lax.axis_size("z")
    tensor_count = lax.axis_size("tensor")
    chips = z_count * tensor_count
    z_index = lax.axis_index("z")
    core_index = lax.axis_index("core")
    tensor_index = lax.axis_index("tensor")
    own_tokens, own_width = hidden.shape
    vocab_rows, full_width = lm_head.shape
    tokens = targets.shape[0]

    sent = jnp.broadcast_to(hidden[None], (chips, own_tokens, own_width))
    got = lax.all_to_all(sent, PLANE, 0, 0, tiled=True)
    both = jnp.stack([got, swap_cores(got)])
    rows = both.reshape(CORES, z_count, tensor_count, own_tokens, own_width)
    rows = rows.transpose(0, 1, 3, 2, 4).reshape(tokens, full_width).astype(jnp.float32)
    inverse = lax.rsqrt(jnp.mean(rows * rows, axis=1) + EPSILON)
    normed = (rows * inverse[:, None] * gain[None, :]).astype(jnp.bfloat16)
    logits = jnp.einsum("td,vd->tv", normed, lm_head, preferred_element_type=jnp.float32)

    by_core = targets.reshape(z_count, CORES, own_tokens)
    row_targets = jnp.where(core_index == 0, by_core, by_core[:, ::-1]).transpose(1, 0, 2).reshape(tokens)
    vocab_start = ((z_index * CORES + core_index) * tensor_count + tensor_index) * vocab_rows
    vocab_ids = vocab_start + jnp.arange(vocab_rows, dtype=jnp.int32)
    is_target = vocab_ids[None, :] == row_targets[:, None]
    allowed = (banned[None, :] == 0) | is_target
    local_max = jnp.max(jnp.where(allowed, logits, LOWEST), axis=1)
    below = logits - local_max[:, None]
    shifted = jnp.where(allowed, jnp.exp(below), 0.0)
    local_sum = jnp.sum(shifted, axis=1)
    local_dot = jnp.sum(jnp.where(allowed, shifted * below, 0.0), axis=1)
    local_target = jnp.sum(jnp.where(is_target, logits, 0.0), axis=1)

    def combine(stats):
        maxima = stats[:, 0]
        top = jnp.max(maxima, axis=0)
        gap = maxima - top[None]
        weight = jnp.exp(gap)
        total = jnp.sum(weight * stats[:, 1], axis=0)
        dot = jnp.sum(weight * (stats[:, 2] + stats[:, 1] * gap), axis=0)
        return jnp.stack([top, total, dot, jnp.sum(stats[:, 3], axis=0)])

    mine = jnp.stack([local_max, local_sum, local_dot, local_target])
    halves = mine.reshape(4, CORES, tokens // CORES)
    theirs = swap_cores(halves[:, ::-1]).reshape(4, tokens)
    pair = combine(jnp.stack([mine, theirs]))
    everyone = lax.all_to_all(jnp.broadcast_to(pair[None], (chips,) + pair.shape), PLANE, 0, 0, tiled=True)

    share = jnp.exp(local_max - pair[0])
    weights = jnp.where(is_target, 0.0, shifted).astype(jnp.bfloat16)
    picks = is_target.astype(jnp.bfloat16)
    head_split = lm_head.reshape(vocab_rows, tensor_count, own_width)

    def split_terms(left, scale):
        terms = jnp.einsum("tv,vkd->tkd", left, head_split, preferred_element_type=jnp.float32)
        if scale is not None:
            terms = terms * scale[:, None, None]
        terms = terms.astype(jnp.bfloat16).reshape(CORES, z_count, own_tokens, tensor_count, own_width)
        return terms.transpose(0, 1, 3, 2, 4)

    terms = jnp.stack([split_terms(weights, share), split_terms(picks, None)], axis=1)
    terms = terms[0].astype(jnp.float32) + swap_cores(terms[1]).astype(jnp.float32)

    top, total, dot, target_logit = combine(everyone)
    loss = top + jnp.log(total) - target_logit
    scale = jnp.exp(pair[0] - top) / total
    target_scale = (jnp.exp(target_logit - top) / total - 1.0).astype(jnp.bfloat16).astype(jnp.float32)
    inner = (dot / total - (target_logit - top)) / full_width

    def by_piece(values):
        return values[: tokens // CORES].reshape(z_count, 1, own_tokens, 1)

    pieces = terms[0] * by_piece(scale) + terms[1] * by_piece(target_scale)
    pieces = pieces.astype(jnp.bfloat16).reshape(chips, own_tokens, own_width)
    grad_normed = jnp.sum(lax.all_to_all(pieces, PLANE, 0, 0, tiled=True).astype(jnp.float32), axis=0)

    def own_rows(values):
        return lax.dynamic_slice_in_dim(values, z_index * own_tokens, own_tokens)

    gain_own = lax.dynamic_slice_in_dim(gain, tensor_index * own_width, own_width)
    inverse_own = own_rows(inverse)[:, None]
    scaled = hidden.astype(jnp.float32) * inverse_own
    gated = grad_normed * gain_own[None, :]
    grad_hidden = (inverse_own * (gated - scaled * own_rows(inner)[:, None])).astype(jnp.bfloat16)
    return (own_rows(loss), grad_hidden)


def solution(mesh):
    dp, pipe, tensor = mesh.devices.shape
    fine = Mesh(mesh.devices.reshape(dp, pipe // CORES, CORES, tensor), ("dp", "z", "core", "tensor"))
    section = ("dp", "z", "core")
    in_specs = (
        P(section, "tensor"),
        P(),
        P(("z", "core", "tensor"), None),
        P("dp"),
        P(("z", "core", "tensor")),
    )
    out_specs = (P(section), P(section, "tensor"))
    return jax.shard_map(local, mesh=fine, in_specs=in_specs, out_specs=out_specs, check_vma=False)
```

```python
import functools
import jax
import jax.numpy as jnp
from jax import lax
from jax.experimental import pallas as pl
from jax.experimental.pallas import tpu as pltpu
from jax.sharding import Mesh
from jax.sharding import PartitionSpec as P

EPSILON = 1e-05
LOWEST = -1e30
CORES = 2
PLANE = ("z", "tensor")
MIB = 1 << 20


def swap_cores(values):
    return lax.ppermute(values, "core", [(0, 1), (1, 0)])


def head_copy(head_ref, chunk_ref, semaphores, y, width):
    columns = pl.ds(pl.multiple_of(y * width, width), width)
    return pltpu.make_async_copy(head_ref.at[:, columns], chunk_ref.at[:, columns], semaphores.at[y])


def swap_halves(row):
    half = row.shape[1] // 2
    return jnp.concatenate([row[:, half:], row[:, :half]], axis=1)


def to_column(row):
    n = row.shape[1]
    square = jnp.broadcast_to(row, (n, n))
    here = lax.broadcasted_iota(jnp.int32, (n, n), 0) == lax.broadcasted_iota(jnp.int32, (n, n), 1)
    return jnp.sum(jnp.where(here, square, 0.0), axis=1, keepdims=True)


def logits_kernel(start_ref, got_ref, swapped_ref, gain_ref, head_ref, targets_ref, banned_ref,
                  lefts_ref, stats_ref, inverse_ref, normed_ref, logits_ref, chunk_ref, semaphores, *, n_z, n_y):
    k, width = got_ref.shape[1:]
    tokens, full_width = normed_ref.shape
    vocab_rows = head_ref.shape[0]
    for y in range(n_y):
        head_copy(head_ref, chunk_ref, semaphores, y, width).start()

    for slot, source in enumerate((got_ref, swapped_ref)):

        @pl.loop(0, n_z // 2)
        def _(pair, slot=slot, source=source):
            first = pair * 2 * n_y
            total = jnp.zeros((2 * k, width), jnp.float32)
            for y in range(n_y):
                block = jnp.concatenate([source[first + y], source[first + n_y + y]], axis=0).astype(jnp.float32)
                total = total + block * block
            inverse = lax.rsqrt(jnp.sum(total, axis=1, keepdims=True) / full_width + EPSILON)
            row = pl.multiple_of(slot * (tokens // 2) + pair * 2 * k, 2 * k)
            inverse_ref[pl.ds(row, 2 * k), :] = jnp.broadcast_to(inverse, (2 * k, inverse_ref.shape[1]))
            for y in range(n_y):
                block = jnp.concatenate([source[first + y], source[first + n_y + y]], axis=0).astype(jnp.float32)
                columns = pl.ds(y * width, width)
                normed_ref[pl.ds(row, 2 * k), columns] = (block * inverse * gain_ref[:, columns]).astype(jnp.bfloat16)

    logits_ref[...] = jnp.zeros_like(logits_ref)

    @pl.loop(0, n_y)
    def _(y):
        head_copy(head_ref, chunk_ref, semaphores, y, width).wait()
        columns = pl.ds(pl.multiple_of(y * width, width), width)
        logits_ref[...] += lax.dot_general(
            chunk_ref[:, columns], normed_ref[:, columns], (((1,), (1,)), ((), ())),
            preferred_element_type=jnp.float32)

    logits = logits_ref[...]
    ids = start_ref[0] + lax.broadcasted_iota(jnp.int32, (vocab_rows, tokens), 0)
    is_target = ids == targets_ref[...]
    allowed = (banned_ref[...] == 0) | is_target
    top = jnp.max(jnp.where(allowed, logits, LOWEST), axis=0, keepdims=True)
    below = logits - top
    shifted = jnp.where(allowed, jnp.exp(below), 0.0)
    total = jnp.sum(shifted, axis=0, keepdims=True)
    dot = jnp.sum(jnp.where(allowed, shifted * below, 0.0), axis=0, keepdims=True)
    target_logit = jnp.sum(jnp.where(is_target, logits, 0.0), axis=0, keepdims=True)
    for i, row in enumerate((top, total, dot, target_logit)):
        stats_ref[0, i : i + 1, :] = row
        stats_ref[1, i : i + 1, :] = swap_halves(row)
    lefts_ref[0] = jnp.where(is_target, 0.0, shifted).T.astype(jnp.bfloat16)
    lefts_ref[1] = is_target.astype(jnp.float32).T.astype(jnp.bfloat16)


def pair_kernel(mine_ref, theirs_ref, out_ref):
    mine, theirs = mine_ref[0], theirs_ref[...]
    top = jnp.maximum(mine[0:1], theirs[0:1])
    total, dot = 0.0, 0.0
    for part in (mine, theirs):
        gap = part[0:1] - top
        weight = jnp.exp(gap)
        total = total + weight * part[1:2]
        dot = dot + weight * (part[2:3] + part[1:2] * gap)
    pair = jnp.concatenate([top, total, dot, mine[3:4] + theirs[3:4]], axis=0)
    out_ref[...] = jnp.broadcast_to(pair[None], out_ref.shape)


def terms_kernel(mine_ref, pair_ref, lefts_ref, head_ref, terms_ref, picks_ref, chunk_ref, semaphores,
                 *, n_z, n_y, slot):
    k, width = picks_ref.shape[-2:]
    half = lefts_ref.shape[1] // 2
    for y in range(n_y):
        head_copy(head_ref, chunk_ref, semaphores, y, width).start()
    here = slice(slot * half, (slot + 1) * half)
    share = to_column(jnp.exp(mine_ref[0, 0:1, :] - pair_ref[0, 0:1, :]))[here]
    lefts = jnp.concatenate([lefts_ref[0, here], lefts_ref[1, here]], axis=0)

    @pl.loop(0, n_y)
    def _(y):
        head_copy(head_ref, chunk_ref, semaphores, y, width).wait()
        columns = pl.ds(pl.multiple_of(y * width, width), width)
        terms = jnp.dot(lefts, chunk_ref[:, columns], preferred_element_type=jnp.float32)
        scaled = terms[:half] * share
        for z in range(n_z):
            rows = slice(z * k, (z + 1) * k)
            terms_ref[z * n_y + y] = scaled[rows].astype(terms_ref.dtype)
            picks_ref[z * n_y + y] = terms[half:][rows].astype(picks_ref.dtype)


def send_kernel(mine_ref, pair_ref, lefts_ref, head_ref, send_ref, chunk_ref, semaphores, *, n_z, n_y):
    terms_kernel(mine_ref, pair_ref, lefts_ref, head_ref, send_ref.at[0], send_ref.at[1], chunk_ref, semaphores,
                 n_z=n_z, n_y=n_y, slot=1)


def keep_kernel(mine_ref, pair_ref, lefts_ref, head_ref, keep_ref, keep_picks_ref, chunk_ref, semaphores, *, n_z, n_y):
    terms_kernel(mine_ref, pair_ref, lefts_ref, head_ref, keep_ref, keep_picks_ref, chunk_ref, semaphores,
                 n_z=n_z, n_y=n_y, slot=0)


def combine_kernel(pair_ref, everyone_ref, loss_ref, columns_ref, *, full_width):
    everyone = everyone_ref[...]
    maxima, sums, dots = everyone[:, 0, :], everyone[:, 1, :], everyone[:, 2, :]
    top = jnp.max(maxima, axis=0, keepdims=True)
    gap = maxima - top
    weight = jnp.exp(gap)
    total = jnp.sum(weight * sums, axis=0, keepdims=True)
    dot = jnp.sum(weight * (dots + sums * gap), axis=0, keepdims=True)
    target_logit = jnp.sum(everyone[:, 3, :], axis=0, keepdims=True)
    loss_ref[...] = jnp.broadcast_to(top + jnp.log(total) - target_logit, loss_ref.shape)
    inner = (dot / total - (target_logit - top)) / full_width
    scale = jnp.exp(pair_ref[0, 0:1, :] - top) / total
    target_scale = (jnp.exp(target_logit - top) / total - 1.0).astype(jnp.bfloat16).astype(jnp.float32)
    lane = lax.broadcasted_iota(jnp.int32, columns_ref.shape, 1)
    columns = jnp.where(lane == 1, to_column(target_scale), to_column(inner))
    columns_ref[...] = jnp.where(lane == 0, to_column(scale), columns)


def pieces_kernel(columns_ref, keep_ref, keep_picks_ref, received_ref, pieces_ref, *, n_z, n_y):
    k, width = keep_ref.shape[1:]

    @pl.loop(0, n_z)
    def _(z):
        rows = pl.ds(pl.multiple_of(z * k, k), k)
        rows_scale = jnp.broadcast_to(columns_ref[rows, 0:1], (k, width))
        picks_scale = jnp.broadcast_to(columns_ref[rows, 1:2], (k, width))
        for y in range(n_y):
            i = z * n_y + y
            terms = keep_ref[i] + received_ref[0, i].astype(jnp.float32)
            picks = keep_picks_ref[i].astype(jnp.float32) + received_ref[1, i].astype(jnp.float32)
            pieces_ref[i] = (terms * rows_scale + picks * picks_scale).astype(jnp.bfloat16)


VMEM = pl.BlockSpec(memory_space=pltpu.VMEM)
HBM = pl.BlockSpec(memory_space=pltpu.HBM)
SMEM = pl.BlockSpec(memory_space=pltpu.SMEM)


def local(hidden, gain, lm_head, targets, banned):
    z_count = lax.axis_size("z")
    tensor_count = lax.axis_size("tensor")
    chips = z_count * tensor_count
    z_index = lax.axis_index("z")
    core_index = lax.axis_index("core")
    tensor_index = lax.axis_index("tensor")
    own_tokens, own_width = hidden.shape
    vocab_rows, full_width = lm_head.shape
    tokens = targets.shape[0]
    f32, bf16 = jnp.float32, jnp.bfloat16
    struct = jax.ShapeDtypeStruct
    head = pltpu.with_memory_space_constraint(lm_head, pltpu.HBM)
    head_scratch = [pltpu.VMEM(lm_head.shape, bf16), pltpu.SemaphoreType.DMA((tensor_count,))]

    by_core = targets.reshape(z_count, CORES, own_tokens)
    row_targets = jnp.where(core_index == 0, by_core, by_core[:, ::-1]).transpose(1, 0, 2).reshape(1, tokens)
    vocab_start = ((z_index * CORES + core_index) * tensor_count + tensor_index) * vocab_rows
    banned_rows = jnp.broadcast_to(banned[:, None], (vocab_rows, tokens))

    sent = jnp.broadcast_to(hidden[None], (chips, own_tokens, own_width))
    got = lax.all_to_all(sent, PLANE, 0, 0, tiled=True)
    swapped = swap_cores(got)

    matmul_flops = 2 * tokens * vocab_rows * full_width
    lefts, mine, inverse = pl.pallas_call(
        functools.partial(logits_kernel, n_z=z_count, n_y=tensor_count),
        out_shape=(struct((2, tokens, vocab_rows), bf16), struct((2, 4, tokens), f32), struct((tokens, 128), f32)),
        in_specs=[SMEM, VMEM, VMEM, VMEM, HBM, VMEM, VMEM],
        out_specs=(VMEM,) * 3,
        scratch_shapes=[pltpu.VMEM((tokens, full_width), bf16), pltpu.VMEM((vocab_rows, tokens), f32)] + head_scratch,
        compiler_params=pltpu.CompilerParams(vmem_limit_bytes=32 * MIB),
        cost_estimate=pl.CostEstimate(flops=matmul_flops, bytes_accessed=12 * MIB, transcendentals=tokens * vocab_rows),
        name="logits",
    )(vocab_start.reshape(1), got, swapped, gain.reshape(1, full_width), head, row_targets, banned_rows)

    theirs = swap_cores(mine[1])
    pair = pl.pallas_call(
        pair_kernel, out_shape=struct((chips, 4, tokens), f32), in_specs=[VMEM] * 2, out_specs=VMEM,
        compiler_params=pltpu.CompilerParams(vmem_limit_bytes=2 * MIB), name="pair",
    )(mine, theirs)
    everyone = lax.all_to_all(pair, PLANE, 0, 0, tiled=True)

    piece = (chips, own_tokens, own_width)
    def half_terms(kernel, out_shape, weight, name):
        return pl.pallas_call(
            functools.partial(kernel, n_z=z_count, n_y=tensor_count),
            out_shape=out_shape,
            in_specs=[VMEM, VMEM, VMEM, HBM],
            out_specs=jax.tree.map(lambda _: VMEM, out_shape),
            scratch_shapes=head_scratch,
            compiler_params=pltpu.CompilerParams(vmem_limit_bytes=32 * MIB),
            cost_estimate=pl.CostEstimate(
                flops=weight * matmul_flops, bytes_accessed=weight * 13 * MIB, transcendentals=0),
            name=name,
        )(mine, pair, lefts, head)

    send = half_terms(send_kernel, struct((2,) + piece, bf16), 1, "send")
    received = swap_cores(send)
    keep, keep_picks = half_terms(keep_kernel, (struct(piece, f32), struct(piece, bf16)), 100, "keep")

    loss, columns = pl.pallas_call(
        functools.partial(combine_kernel, full_width=full_width),
        out_shape=(struct((8, tokens), f32), struct((tokens, 128), f32)),
        in_specs=[VMEM] * 2,
        out_specs=(VMEM,) * 2,
        compiler_params=pltpu.CompilerParams(vmem_limit_bytes=4 * MIB),
        cost_estimate=pl.CostEstimate(flops=0, bytes_accessed=32 * MIB, transcendentals=0),
        name="combine",
    )(pair, everyone)
    pieces = pl.pallas_call(
        functools.partial(pieces_kernel, n_z=z_count, n_y=tensor_count),
        out_shape=struct(piece, bf16),
        in_specs=[VMEM] * 4,
        out_specs=VMEM,
        compiler_params=pltpu.CompilerParams(vmem_limit_bytes=16 * MIB),
        cost_estimate=pl.CostEstimate(flops=0, bytes_accessed=8 * MIB, transcendentals=0),
        name="pieces",
    )(columns, keep, keep_picks, received)
    grad_normed = jnp.sum(lax.all_to_all(pieces, PLANE, 0, 0, tiled=True).astype(f32), axis=0)

    def own_rows(values):
        return lax.dynamic_slice_in_dim(values, z_index * own_tokens, own_tokens)

    gain_own = lax.dynamic_slice_in_dim(gain, tensor_index * own_width, own_width)
    inverse_own = own_rows(inverse)[:, :1]
    scaled = hidden.astype(f32) * inverse_own
    gated = grad_normed * gain_own[None, :]
    grad_hidden = (inverse_own * (gated - scaled * own_rows(columns)[:, 2:3])).astype(bf16)
    return (own_rows(loss[0]), grad_hidden)


def solution(mesh):
    dp, pipe, tensor = mesh.devices.shape
    fine = Mesh(mesh.devices.reshape(dp, pipe // CORES, CORES, tensor), ("dp", "z", "core", "tensor"))
    section = ("dp", "z", "core")
    in_specs = (
        P(section, "tensor"),
        P(),
        P(("z", "core", "tensor"), None),
        P("dp"),
        P(("z", "core", "tensor")),
    )
    out_specs = (P(section), P(section, "tensor"))
    return jax.shard_map(local, mesh=fine, in_specs=in_specs, out_specs=out_specs, check_vma=False)
```

```python
import functools
import jax
import jax.numpy as jnp
from jax import lax
from jax.experimental import pallas as pl
from jax.experimental.pallas import tpu as pltpu
from jax.sharding import Mesh
from jax.sharding import PartitionSpec as P

EPSILON = 1e-05
LOWEST = -1e30
CORES = 2
PLANE = ("z", "tensor")
MIB = 1 << 20


def swap_cores(values):
    return lax.ppermute(values, "core", [(0, 1), (1, 0)])


def head_copy(head_ref, chunk_ref, semaphores, y, width):
    columns = pl.ds(pl.multiple_of(y * width, width), width)
    return pltpu.make_async_copy(head_ref.at[:, columns], chunk_ref.at[:, columns], semaphores.at[y])


def swap_halves(row):
    half = row.shape[1] // 2
    return jnp.concatenate([row[:, half:], row[:, :half]], axis=1)


def to_column(row):
    n = row.shape[1]
    square = jnp.broadcast_to(row, (n, n))
    here = lax.broadcasted_iota(jnp.int32, (n, n), 0) == lax.broadcasted_iota(jnp.int32, (n, n), 1)
    return jnp.sum(jnp.where(here, square, 0.0), axis=1, keepdims=True)


def logits_kernel(start_ref, got_ref, swapped_ref, gain_ref, head_ref, targets_ref, banned_ref,
                  lefts_ref, stats_ref, inverse_ref, chunk_ref, normed_ref, logits_ref, semaphores, *, n_z, n_y):
    k, width = got_ref.shape[1:]
    tokens, full_width = normed_ref.shape
    vocab_rows = head_ref.shape[0]
    for y in range(n_y):
        head_copy(head_ref, chunk_ref, semaphores, y, width).start()

    for slot, source in enumerate((got_ref, swapped_ref)):

        @pl.loop(0, n_z // 2)
        def _(pair, slot=slot, source=source):
            first = pair * 2 * n_y
            total = jnp.zeros((2 * k, width), jnp.float32)
            for y in range(n_y):
                block = jnp.concatenate([source[first + y], source[first + n_y + y]], axis=0).astype(jnp.float32)
                total = total + block * block
            inverse = lax.rsqrt(jnp.sum(total, axis=1, keepdims=True) / full_width + EPSILON)
            row = pl.multiple_of(slot * (tokens // 2) + pair * 2 * k, 2 * k)
            inverse_ref[pl.ds(row, 2 * k), :] = jnp.broadcast_to(inverse, (2 * k, inverse_ref.shape[1]))
            for y in range(n_y):
                block = jnp.concatenate([source[first + y], source[first + n_y + y]], axis=0).astype(jnp.float32)
                columns = pl.ds(y * width, width)
                normed_ref[pl.ds(row, 2 * k), columns] = (block * inverse * gain_ref[:, columns]).astype(jnp.bfloat16)

    logits_ref[...] = jnp.zeros_like(logits_ref)

    @pl.loop(0, n_y)
    def _(y):
        head_copy(head_ref, chunk_ref, semaphores, y, width).wait()
        columns = pl.ds(pl.multiple_of(y * width, width), width)
        logits_ref[...] += lax.dot_general(
            chunk_ref[:, columns], normed_ref[:, columns], (((1,), (1,)), ((), ())),
            preferred_element_type=jnp.float32)

    logits = logits_ref[...]
    ids = start_ref[0] + lax.broadcasted_iota(jnp.int32, (vocab_rows, tokens), 0)
    is_target = ids == targets_ref[...]
    allowed = (banned_ref[...] == 0) | is_target
    top = jnp.max(jnp.where(allowed, logits, LOWEST), axis=0, keepdims=True)
    below = logits - top
    shifted = jnp.where(allowed, jnp.exp(below), 0.0)
    total = jnp.sum(shifted, axis=0, keepdims=True)
    dot = jnp.sum(jnp.where(allowed, shifted * below, 0.0), axis=0, keepdims=True)
    target_logit = jnp.sum(jnp.where(is_target, logits, 0.0), axis=0, keepdims=True)
    for i, row in enumerate((top, total, dot, target_logit)):
        stats_ref[0, i : i + 1, :] = row
        stats_ref[1, i : i + 1, :] = swap_halves(row)
    lefts_ref[:tokens, :] = jnp.where(is_target, 0.0, shifted).T.astype(jnp.bfloat16)
    lefts_ref[tokens:, :] = is_target.astype(jnp.float32).T.astype(jnp.bfloat16)


def pair_kernel(mine_ref, theirs_ref, out_ref):
    mine, theirs = mine_ref[0], theirs_ref[...]
    top = jnp.maximum(mine[0:1], theirs[0:1])
    total, dot = 0.0, 0.0
    for part in (mine, theirs):
        gap = part[0:1] - top
        weight = jnp.exp(gap)
        total = total + weight * part[1:2]
        dot = dot + weight * (part[2:3] + part[1:2] * gap)
    pair = jnp.concatenate([top, total, dot, mine[3:4] + theirs[3:4]], axis=0)
    out_ref[...] = jnp.broadcast_to(pair[None], out_ref.shape)


def terms_kernel(mine_ref, pair_ref, lefts_ref, head_ref, send_ref, keep_ref, keep_picks_ref, *, n_z, n_y):
    k, width = keep_ref.shape[1:]
    tokens = lefts_ref.shape[0] // 2
    half = tokens // 2
    share = to_column(jnp.exp(mine_ref[0, 0:1, :] - pair_ref[0, 0:1, :]))

    @pl.loop(0, n_y)
    def _(y):
        columns = pl.ds(pl.multiple_of(y * width, width), width)
        terms = jnp.dot(lefts_ref[...], head_ref[:, columns], preferred_element_type=jnp.float32)
        scaled = terms[:tokens] * share
        for z in range(n_z):
            own = slice(z * k, (z + 1) * k)
            other = slice(half + z * k, half + (z + 1) * k)
            keep_ref[z * n_y + y] = scaled[own]
            send_ref[0, z * n_y + y] = scaled[other].astype(jnp.bfloat16)
            keep_picks_ref[z * n_y + y] = terms[tokens:][own].astype(jnp.bfloat16)
            send_ref[1, z * n_y + y] = terms[tokens:][other].astype(jnp.bfloat16)


def combine_kernel(pair_ref, everyone_ref, loss_ref, columns_ref, *, full_width):
    everyone = everyone_ref[...]
    maxima, sums, dots = everyone[:, 0, :], everyone[:, 1, :], everyone[:, 2, :]
    top = jnp.max(maxima, axis=0, keepdims=True)
    gap = maxima - top
    weight = jnp.exp(gap)
    total = jnp.sum(weight * sums, axis=0, keepdims=True)
    dot = jnp.sum(weight * (dots + sums * gap), axis=0, keepdims=True)
    target_logit = jnp.sum(everyone[:, 3, :], axis=0, keepdims=True)
    loss_ref[...] = jnp.broadcast_to(top + jnp.log(total) - target_logit, loss_ref.shape)
    inner = (dot / total - (target_logit - top)) / full_width
    scale = jnp.exp(pair_ref[0, 0:1, :] - top) / total
    target_scale = (jnp.exp(target_logit - top) / total - 1.0).astype(jnp.bfloat16).astype(jnp.float32)
    lane = lax.broadcasted_iota(jnp.int32, columns_ref.shape, 1)
    columns = jnp.where(lane == 1, to_column(target_scale), to_column(inner))
    columns_ref[...] = jnp.where(lane == 0, to_column(scale), columns)


def pieces_kernel(columns_ref, keep_ref, keep_picks_ref, received_ref, pieces_ref, *, n_z, n_y):
    k, width = keep_ref.shape[1:]

    @pl.loop(0, n_z)
    def _(z):
        rows = pl.ds(pl.multiple_of(z * k, k), k)
        rows_scale = jnp.broadcast_to(columns_ref[rows, 0:1], (k, width))
        picks_scale = jnp.broadcast_to(columns_ref[rows, 1:2], (k, width))
        for y in range(n_y):
            i = z * n_y + y
            terms = keep_ref[i] + received_ref[0, i].astype(jnp.float32)
            picks = keep_picks_ref[i].astype(jnp.float32) + received_ref[1, i].astype(jnp.float32)
            pieces_ref[i] = (terms * rows_scale + picks * picks_scale).astype(jnp.bfloat16)


VMEM = pl.BlockSpec(memory_space=pltpu.VMEM)
HBM = pl.BlockSpec(memory_space=pltpu.HBM)
SMEM = pl.BlockSpec(memory_space=pltpu.SMEM)


def local(hidden, gain, lm_head, targets, banned):
    z_count = lax.axis_size("z")
    tensor_count = lax.axis_size("tensor")
    chips = z_count * tensor_count
    z_index = lax.axis_index("z")
    core_index = lax.axis_index("core")
    tensor_index = lax.axis_index("tensor")
    own_tokens, own_width = hidden.shape
    vocab_rows, full_width = lm_head.shape
    tokens = targets.shape[0]
    f32, bf16 = jnp.float32, jnp.bfloat16
    struct = jax.ShapeDtypeStruct
    head = pltpu.with_memory_space_constraint(lm_head, pltpu.HBM)

    by_core = targets.reshape(z_count, CORES, own_tokens)
    row_targets = jnp.where(core_index == 0, by_core, by_core[:, ::-1]).transpose(1, 0, 2).reshape(1, tokens)
    vocab_start = ((z_index * CORES + core_index) * tensor_count + tensor_index) * vocab_rows
    banned_rows = jnp.broadcast_to(banned[:, None], (vocab_rows, tokens))

    sent = jnp.broadcast_to(hidden[None], (chips, own_tokens, own_width))
    got = lax.all_to_all(sent, PLANE, 0, 0, tiled=True)
    swapped = swap_cores(got)

    matmul_flops = 2 * tokens * vocab_rows * full_width
    lefts, mine, inverse, on_chip = pl.pallas_call(
        functools.partial(logits_kernel, n_z=z_count, n_y=tensor_count),
        out_shape=(struct((2 * tokens, vocab_rows), bf16), struct((2, 4, tokens), f32), struct((tokens, 128), f32),
                   struct(lm_head.shape, bf16)),
        in_specs=[SMEM, VMEM, VMEM, VMEM, HBM, VMEM, VMEM],
        out_specs=(VMEM,) * 4,
        scratch_shapes=[pltpu.VMEM((tokens, full_width), bf16), pltpu.VMEM((vocab_rows, tokens), f32),
                        pltpu.SemaphoreType.DMA((tensor_count,))],
        compiler_params=pltpu.CompilerParams(vmem_limit_bytes=24 * MIB),
        cost_estimate=pl.CostEstimate(flops=matmul_flops, bytes_accessed=12 * MIB, transcendentals=tokens * vocab_rows),
        name="logits",
    )(vocab_start.reshape(1), got, swapped, gain.reshape(1, full_width), head, row_targets, banned_rows)

    theirs = swap_cores(mine[1])
    pair = pl.pallas_call(
        pair_kernel, out_shape=struct((chips, 4, tokens), f32), in_specs=[VMEM] * 2, out_specs=VMEM,
        compiler_params=pltpu.CompilerParams(vmem_limit_bytes=2 * MIB), name="pair",
    )(mine, theirs)
    everyone = lax.all_to_all(pair, PLANE, 0, 0, tiled=True)

    piece = (chips, own_tokens, own_width)
    send, keep, keep_picks = pl.pallas_call(
        functools.partial(terms_kernel, n_z=z_count, n_y=tensor_count),
        out_shape=(struct((2,) + piece, bf16), struct(piece, f32), struct(piece, bf16)),
        in_specs=[VMEM] * 4,
        out_specs=(VMEM,) * 3,
        compiler_params=pltpu.CompilerParams(vmem_limit_bytes=24 * MIB),
        cost_estimate=pl.CostEstimate(flops=2 * matmul_flops, bytes_accessed=16 * MIB, transcendentals=0),
        name="terms",
    )(mine, pair, lefts, on_chip)
    received = swap_cores(send)

    loss, columns = pl.pallas_call(
        functools.partial(combine_kernel, full_width=full_width),
        out_shape=(struct((8, tokens), f32), struct((tokens, 128), f32)),
        in_specs=[VMEM] * 2,
        out_specs=(VMEM,) * 2,
        compiler_params=pltpu.CompilerParams(vmem_limit_bytes=4 * MIB),
        cost_estimate=pl.CostEstimate(flops=0, bytes_accessed=32 * MIB, transcendentals=0),
        name="combine",
    )(pair, everyone)
    pieces = pl.pallas_call(
        functools.partial(pieces_kernel, n_z=z_count, n_y=tensor_count),
        out_shape=struct(piece, bf16),
        in_specs=[VMEM] * 4,
        out_specs=VMEM,
        compiler_params=pltpu.CompilerParams(vmem_limit_bytes=16 * MIB),
        cost_estimate=pl.CostEstimate(flops=0, bytes_accessed=8 * MIB, transcendentals=0),
        name="pieces",
    )(columns, keep, keep_picks, received)
    grad_normed = jnp.sum(lax.all_to_all(pieces, PLANE, 0, 0, tiled=True).astype(f32), axis=0)

    def own_rows(values):
        return lax.dynamic_slice_in_dim(values, z_index * own_tokens, own_tokens)

    gain_own = lax.dynamic_slice_in_dim(gain, tensor_index * own_width, own_width)
    inverse_own = own_rows(inverse)[:, :1]
    scaled = hidden.astype(f32) * inverse_own
    gated = grad_normed * gain_own[None, :]
    grad_hidden = (inverse_own * (gated - scaled * own_rows(columns)[:, 2:3])).astype(bf16)
    return (own_rows(loss[0]), grad_hidden)


def solution(mesh):
    dp, pipe, tensor = mesh.devices.shape
    fine = Mesh(mesh.devices.reshape(dp, pipe // CORES, CORES, tensor), ("dp", "z", "core", "tensor"))
    section = ("dp", "z", "core")
    in_specs = (
        P(section, "tensor"),
        P(),
        P(("z", "core", "tensor"), None),
        P("dp"),
        P(("z", "core", "tensor")),
    )
    out_specs = (P(section), P(section, "tensor"))
    return jax.shard_map(local, mesh=fine, in_specs=in_specs, out_specs=out_specs, check_vma=False)
```

```python
import functools
import jax
import jax.numpy as jnp
from jax import lax
from jax.experimental import pallas as pl
from jax.experimental.pallas import tpu as pltpu
from jax.sharding import Mesh
from jax.sharding import PartitionSpec as P

EPSILON = 1e-05
LOWEST = -1e30
CORES = 2
PLANE = ("z", "tensor")
MIB = 1 << 20


def swap_cores(values):
    return lax.ppermute(values, "core", [(0, 1), (1, 0)])


def head_copy(head_ref, chunk_ref, semaphores, y, width):
    columns = pl.ds(pl.multiple_of(y * width, width), width)
    return pltpu.make_async_copy(head_ref.at[:, columns], chunk_ref.at[:, columns], semaphores.at[y])


def swap_halves(row):
    half = row.shape[1] // 2
    return jnp.concatenate([row[:, half:], row[:, :half]], axis=1)


def to_column(row):
    n = row.shape[1]
    square = jnp.broadcast_to(row, (n, n))
    here = lax.broadcasted_iota(jnp.int32, (n, n), 0) == lax.broadcasted_iota(jnp.int32, (n, n), 1)
    return jnp.sum(jnp.where(here, square, jnp.zeros_like(square)), axis=1, keepdims=True)


def to_row(column):
    n = column.shape[0]
    square = jnp.broadcast_to(column, (n, n))
    here = lax.broadcasted_iota(jnp.int32, (n, n), 0) == lax.broadcasted_iota(jnp.int32, (n, n), 1)
    return jnp.sum(jnp.where(here, square, 0.0), axis=0, keepdims=True)


def logits_kernel(start_ref, got_ref, swapped_ref, gain_ref, head_ref, targets_ref, banned_ref,
                  lefts_ref, stats_ref, inverse_ref, chunk_ref, normed_ref, logits_ref, semaphores, *, n_z, n_y):
    k, width = got_ref.shape[1:]
    tokens, full_width = normed_ref.shape
    vocab_rows = head_ref.shape[0]
    for y in range(n_y):
        head_copy(head_ref, chunk_ref, semaphores, y, width).start()

    for slot, source in enumerate((got_ref, swapped_ref)):

        @pl.loop(0, n_z // 2)
        def _(pair, slot=slot, source=source):
            first = pair * 2 * n_y
            total = jnp.zeros((2 * k, width), jnp.float32)
            for y in range(n_y):
                block = jnp.concatenate([source[first + y], source[first + n_y + y]], axis=0).astype(jnp.float32)
                total = total + block * block
            inverse = lax.rsqrt(jnp.sum(total, axis=1, keepdims=True) / full_width + EPSILON)
            row = pl.multiple_of(slot * (tokens // 2) + pair * 2 * k, 2 * k)
            inverse_ref[pl.ds(row, 2 * k), :] = jnp.broadcast_to(inverse, (2 * k, inverse_ref.shape[1]))
            for y in range(n_y):
                block = jnp.concatenate([source[first + y], source[first + n_y + y]], axis=0).astype(jnp.float32)
                columns = pl.ds(y * width, width)
                normed_ref[pl.ds(row, 2 * k), columns] = (block * inverse * gain_ref[:, columns]).astype(jnp.bfloat16)

    logits_ref[...] = jnp.zeros_like(logits_ref)

    @pl.loop(0, n_y)
    def _(y):
        head_copy(head_ref, chunk_ref, semaphores, y, width).wait()
        columns = pl.ds(pl.multiple_of(y * width, width), width)
        logits_ref[...] += lax.dot_general(
            normed_ref[:, columns], chunk_ref[:, columns], (((1,), (1,)), ((), ())),
            preferred_element_type=jnp.float32)

    logits = logits_ref[...]
    ids = start_ref[0] + lax.broadcasted_iota(jnp.int32, (tokens, vocab_rows), 1)
    is_target = ids == to_column(targets_ref[...])
    allowed = (banned_ref[...] == 0) | is_target
    top = jnp.max(jnp.where(allowed, logits, LOWEST), axis=1, keepdims=True)
    below = logits - top
    shifted = jnp.where(allowed, jnp.exp(below), 0.0)
    total = jnp.sum(shifted, axis=1, keepdims=True)
    dot = jnp.sum(jnp.where(allowed, shifted * below, 0.0), axis=1, keepdims=True)
    target_logit = jnp.sum(jnp.where(is_target, logits, 0.0), axis=1, keepdims=True)
    for i, column in enumerate((top, total, dot, target_logit)):
        row = to_row(column)
        stats_ref[0, i : i + 1, :] = row
        stats_ref[1, i : i + 1, :] = swap_halves(row)
    lefts_ref[:tokens, :] = jnp.where(is_target, 0.0, shifted).astype(jnp.bfloat16)
    lefts_ref[tokens:, :] = is_target.astype(jnp.float32).astype(jnp.bfloat16)


def pair_kernel(mine_ref, theirs_ref, out_ref):
    mine, theirs = mine_ref[0], theirs_ref[...]
    top = jnp.maximum(mine[0:1], theirs[0:1])
    total, dot = 0.0, 0.0
    for part in (mine, theirs):
        gap = part[0:1] - top
        weight = jnp.exp(gap)
        total = total + weight * part[1:2]
        dot = dot + weight * (part[2:3] + part[1:2] * gap)
    pair = jnp.concatenate([top, total, dot, mine[3:4] + theirs[3:4]], axis=0)
    out_ref[...] = jnp.broadcast_to(pair[None], out_ref.shape)


def terms_kernel(mine_ref, pair_ref, lefts_ref, head_ref, send_ref, keep_ref, keep_picks_ref, *, n_z, n_y):
    k, width = keep_ref.shape[1:]
    tokens = lefts_ref.shape[0] // 2
    half = tokens // 2
    share = to_column(jnp.exp(mine_ref[0, 0:1, :] - pair_ref[0, 0:1, :]))

    @pl.loop(0, n_y)
    def _(y):
        columns = pl.ds(pl.multiple_of(y * width, width), width)
        terms = jnp.dot(lefts_ref[...], head_ref[:, columns], preferred_element_type=jnp.float32)
        scaled = terms[:tokens] * share
        for z in range(n_z):
            own = slice(z * k, (z + 1) * k)
            other = slice(half + z * k, half + (z + 1) * k)
            keep_ref[z * n_y + y] = scaled[own]
            send_ref[0, z * n_y + y] = scaled[other].astype(jnp.bfloat16)
            keep_picks_ref[z * n_y + y] = terms[tokens:][own].astype(jnp.bfloat16)
            send_ref[1, z * n_y + y] = terms[tokens:][other].astype(jnp.bfloat16)


def combine_kernel(pair_ref, everyone_ref, loss_ref, columns_ref, *, full_width):
    everyone = everyone_ref[...]
    maxima, sums, dots = everyone[:, 0, :], everyone[:, 1, :], everyone[:, 2, :]
    top = jnp.max(maxima, axis=0, keepdims=True)
    gap = maxima - top
    weight = jnp.exp(gap)
    total = jnp.sum(weight * sums, axis=0, keepdims=True)
    dot = jnp.sum(weight * (dots + sums * gap), axis=0, keepdims=True)
    target_logit = jnp.sum(everyone[:, 3, :], axis=0, keepdims=True)
    loss_ref[...] = jnp.broadcast_to(top + jnp.log(total) - target_logit, loss_ref.shape)
    inner = (dot / total - (target_logit - top)) / full_width
    scale = jnp.exp(pair_ref[0, 0:1, :] - top) / total
    target_scale = (jnp.exp(target_logit - top) / total - 1.0).astype(jnp.bfloat16).astype(jnp.float32)
    lane = lax.broadcasted_iota(jnp.int32, columns_ref.shape, 1)
    columns = jnp.where(lane == 1, to_column(target_scale), to_column(inner))
    columns_ref[...] = jnp.where(lane == 0, to_column(scale), columns)


def pieces_kernel(columns_ref, keep_ref, keep_picks_ref, received_ref, pieces_ref, *, n_z, n_y):
    k, width = keep_ref.shape[1:]

    @pl.loop(0, n_z)
    def _(z):
        rows = pl.ds(pl.multiple_of(z * k, k), k)
        rows_scale = jnp.broadcast_to(columns_ref[rows, 0:1], (k, width))
        picks_scale = jnp.broadcast_to(columns_ref[rows, 1:2], (k, width))
        for y in range(n_y):
            i = z * n_y + y
            terms = keep_ref[i] + received_ref[0, i].astype(jnp.float32)
            picks = keep_picks_ref[i].astype(jnp.float32) + received_ref[1, i].astype(jnp.float32)
            pieces_ref[i] = (terms * rows_scale + picks * picks_scale).astype(jnp.bfloat16)


VMEM = pl.BlockSpec(memory_space=pltpu.VMEM)
HBM = pl.BlockSpec(memory_space=pltpu.HBM)
SMEM = pl.BlockSpec(memory_space=pltpu.SMEM)


def local(hidden, gain, lm_head, targets, banned):
    z_count = lax.axis_size("z")
    tensor_count = lax.axis_size("tensor")
    chips = z_count * tensor_count
    z_index = lax.axis_index("z")
    core_index = lax.axis_index("core")
    tensor_index = lax.axis_index("tensor")
    own_tokens, own_width = hidden.shape
    vocab_rows, full_width = lm_head.shape
    tokens = targets.shape[0]
    f32, bf16 = jnp.float32, jnp.bfloat16
    struct = jax.ShapeDtypeStruct
    head = pltpu.with_memory_space_constraint(lm_head, pltpu.HBM)

    by_core = targets.reshape(z_count, CORES, own_tokens)
    row_targets = jnp.where(core_index == 0, by_core, by_core[:, ::-1]).transpose(1, 0, 2).reshape(1, tokens)
    vocab_start = ((z_index * CORES + core_index) * tensor_count + tensor_index) * vocab_rows
    banned_rows = banned.reshape(1, vocab_rows)

    sent = jnp.broadcast_to(hidden[None], (chips, own_tokens, own_width))
    got = lax.all_to_all(sent, PLANE, 0, 0, tiled=True)
    swapped = swap_cores(got)

    matmul_flops = 2 * tokens * vocab_rows * full_width
    lefts, mine, inverse, on_chip = pl.pallas_call(
        functools.partial(logits_kernel, n_z=z_count, n_y=tensor_count),
        out_shape=(struct((2 * tokens, vocab_rows), bf16), struct((2, 4, tokens), f32), struct((tokens, 128), f32),
                   struct(lm_head.shape, bf16)),
        in_specs=[SMEM, VMEM, VMEM, VMEM, HBM, VMEM, VMEM],
        out_specs=(VMEM,) * 4,
        scratch_shapes=[pltpu.VMEM((tokens, full_width), bf16), pltpu.VMEM((tokens, vocab_rows), f32),
                        pltpu.SemaphoreType.DMA((tensor_count,))],
        compiler_params=pltpu.CompilerParams(vmem_limit_bytes=24 * MIB),
        cost_estimate=pl.CostEstimate(flops=matmul_flops, bytes_accessed=12 * MIB, transcendentals=tokens * vocab_rows),
        name="logits",
    )(vocab_start.reshape(1), got, swapped, gain.reshape(1, full_width), head, row_targets, banned_rows)

    theirs = swap_cores(mine[1])
    pair = pl.pallas_call(
        pair_kernel, out_shape=struct((chips, 4, tokens), f32), in_specs=[VMEM] * 2, out_specs=VMEM,
        compiler_params=pltpu.CompilerParams(vmem_limit_bytes=2 * MIB), name="pair",
    )(mine, theirs)
    everyone = lax.all_to_all(pair, PLANE, 0, 0, tiled=True)

    piece = (chips, own_tokens, own_width)
    send, keep, keep_picks = pl.pallas_call(
        functools.partial(terms_kernel, n_z=z_count, n_y=tensor_count),
        out_shape=(struct((2,) + piece, bf16), struct(piece, f32), struct(piece, bf16)),
        in_specs=[VMEM] * 4,
        out_specs=(VMEM,) * 3,
        compiler_params=pltpu.CompilerParams(vmem_limit_bytes=24 * MIB),
        cost_estimate=pl.CostEstimate(flops=2 * matmul_flops, bytes_accessed=16 * MIB, transcendentals=0),
        name="terms",
    )(mine, pair, lefts, on_chip)
    received = swap_cores(send)

    loss, columns = pl.pallas_call(
        functools.partial(combine_kernel, full_width=full_width),
        out_shape=(struct((8, tokens), f32), struct((tokens, 128), f32)),
        in_specs=[VMEM] * 2,
        out_specs=(VMEM,) * 2,
        compiler_params=pltpu.CompilerParams(vmem_limit_bytes=4 * MIB),
        cost_estimate=pl.CostEstimate(flops=0, bytes_accessed=32 * MIB, transcendentals=0),
        name="combine",
    )(pair, everyone)
    pieces = pl.pallas_call(
        functools.partial(pieces_kernel, n_z=z_count, n_y=tensor_count),
        out_shape=struct(piece, bf16),
        in_specs=[VMEM] * 4,
        out_specs=VMEM,
        compiler_params=pltpu.CompilerParams(vmem_limit_bytes=16 * MIB),
        cost_estimate=pl.CostEstimate(flops=0, bytes_accessed=8 * MIB, transcendentals=0),
        name="pieces",
    )(columns, keep, keep_picks, received)
    grad_normed = jnp.sum(lax.all_to_all(pieces, PLANE, 0, 0, tiled=True).astype(f32), axis=0)

    def own_rows(values):
        return lax.dynamic_slice_in_dim(values, z_index * own_tokens, own_tokens)

    gain_own = lax.dynamic_slice_in_dim(gain, tensor_index * own_width, own_width)
    inverse_own = own_rows(inverse)[:, :1]
    scaled = hidden.astype(f32) * inverse_own
    gated = grad_normed * gain_own[None, :]
    grad_hidden = (inverse_own * (gated - scaled * own_rows(columns)[:, 2:3])).astype(bf16)
    return (own_rows(loss[0]), grad_hidden)


def solution(mesh):
    dp, pipe, tensor = mesh.devices.shape
    fine = Mesh(mesh.devices.reshape(dp, pipe // CORES, CORES, tensor), ("dp", "z", "core", "tensor"))
    section = ("dp", "z", "core")
    in_specs = (
        P(section, "tensor"),
        P(),
        P(("z", "core", "tensor"), None),
        P("dp"),
        P(("z", "core", "tensor")),
    )
    out_specs = (P(section), P(section, "tensor"))
    return jax.shard_map(local, mesh=fine, in_specs=in_specs, out_specs=out_specs, check_vma=False)
```
